32 devices in a mesh: grp: 2 (over x), ctx: 16 (over z, y, core).
Axes of the slice: x: 2, y: 2, z: 4, core: 2. Of those that a mesh axis runs over, the one named last changes fastest.
Arguments:
- queries: bfloat16 [16384, 2048], P(('grp', 'ctx')), parts along dimension 0, may hold values from -7 to 7
- keys: bfloat16 [16384, 512], P(('grp', 'ctx')), parts along dimension 0, may hold values from -6 to 6
- values: bfloat16 [16384, 512], P(('grp', 'ctx')), parts along dimension 0, may hold values from -6 to 6
- out_grad: bfloat16 [16384, 2048], P(('grp', 'ctx')), parts along dimension 0, may hold values from -6 to 6
- doc_starts: int32 [16], P('grp'), parts along dimension 0, may hold values from 0 to 7423, as said below
- block_lists: int32 [128, 6], P(('grp', 'ctx')), parts along dimension 0, may hold values from -1 to 63, as said below
Outputs:
- attended: bfloat16 [16384, 2048], P(('grp', 'ctx')), parts along dimension 0
- grad_queries: bfloat16 [16384, 2048], P(('grp', 'ctx')), parts along dimension 0
- grad_keys: bfloat16 [16384, 512], P(('grp', 'ctx')), parts along dimension 0
- grad_values: bfloat16 [16384, 512], P(('grp', 'ctx')), parts along dimension 0
The draws below stay inside these ranges and needn't reach their ends.
There are 2 independent parts, one for each index of `grp`. The reference program is written for one: setup_inputs(seed, part) draws one part's arguments, and reference() takes and returns one part's arrays. A program takes and returns all parts, laid end to end along the dimension named above; each array names one. Nothing has to cross between parts.
Inputs may be any that keep to these rules, and one draw needn't show every extreme that they name: `block_lists`: row b lists block b first, then further distinct blocks before b that lie in the document of b's last token and among the blocks of b's device or of the 2 devices before it, then -1 in every slot left empty; the last row is full. `doc_starts`: Increasing, the first entry 0.
All inputs are finite; a program needn't handle non-finite values.
Results may differ from the reference program's by a relative error of at most 0.029.
Values may be sent and summed in bfloat16 or wider, within the bound.
No kernel may reach another device: no remote copies, remote signals or barrier semaphores. Data moves between devices by JAX's collectives and lax.ppermute only.
A program may use at most 128 MiB of HBM per device.

```python
import jax
import jax.numpy as jnp
from jax import lax

HD = 128
HEADS = 16
KV_HEADS = 4
BLOCK = 128
BLK_DEV = 4
LIST = 6
R_DEV = 2
DOCS = 8
SEQ = 8192
NBLK = 64


def doc_and_lists(key):
    base = jax.random.fold_in(key, 101)
    start_key, score_key, count_key = jax.random.split(base, 3)
    span = SEQ // DOCS
    shake = span // 4
    order = jnp.arange(DOCS, dtype=jnp.int32)
    jitter = jax.random.randint(start_key, (DOCS,), -shake, shake)
    starts = jnp.where(order == 0, 0, order * span + jitter).astype(jnp.int32)
    blocks_all = jnp.arange(NBLK, dtype=jnp.int32)
    last_token = blocks_all * BLOCK + BLOCK - 1
    doc_last = jnp.sum((last_token[:, None] >= starts[None, 1:]).astype(jnp.int32), axis=1)
    doc_first = jnp.sum(jnp.where(doc_last[:, None] == order[None, :], starts[None, :], 0), axis=1)
    lowest = jnp.maximum(doc_first // BLOCK, (blocks_all // BLK_DEV - R_DEV) * BLK_DEV)
    lowest = jnp.maximum(lowest, 0)
    available = blocks_all - lowest + 1
    wanted = jax.random.randint(count_key, (NBLK,), 2, LIST + 1)
    live_count = jnp.minimum(available, wanted)
    live_count = jnp.where(blocks_all == NBLK - 1, jnp.minimum(available, LIST), live_count)
    reach_back = (R_DEV + 1) * BLK_DEV - 1
    backward = jnp.arange(1, reach_back + 1, dtype=jnp.int32)
    candidates = blocks_all[:, None] - backward[None, :]
    noise = jax.random.randint(score_key, (NBLK, reach_back), 0, 65536)
    ranking = jnp.where(candidates >= lowest[:, None], noise * 64 + backward[None, :], -1 - backward[None, :])
    top_values, top_index = lax.top_k(ranking, LIST - 1)
    chosen = blocks_all[:, None] - (top_index.astype(jnp.int32) + 1)
    slot_ids = jnp.arange(1, LIST, dtype=jnp.int32)
    remaining = jnp.where(slot_ids[None, :] < live_count[:, None], chosen, -1)
    lists = jnp.concatenate([blocks_all[:, None], remaining], axis=1).astype(jnp.int32)
    return (starts, lists)


def draw_doc_starts(key, part):
    return doc_and_lists(key)[0]


def draw_block_lists(key, part):
    return doc_and_lists(key)[1]


def drawn_pair(key):
    base = jax.random.fold_in(key, 202)
    query_key, key_key = jax.random.split(base, 2)
    queries = jnp.clip(jax.random.normal(query_key, (SEQ, HEADS * HD), jnp.float32), -6.0, 6.0)
    keys = jnp.clip(jax.random.normal(key_key, (SEQ, KV_HEADS * HD), jnp.float32), -6.0, 6.0)
    return (queries, keys)


def draw_queries(key, part):
    return drawn_pair(key)[0].astype(jnp.bfloat16)


def draw_keys(key, part):
    return drawn_pair(key)[1].astype(jnp.bfloat16)


def steps_of(rng, shape, pieces, least, high):
    def one(axis_at, blocks):
        heights = jax.random.uniform(jax.random.fold_in(jax.random.fold_in(rng, 6), axis_at), (blocks,), jnp.float32, least / len(pieces), high / len(pieces))
        return jnp.repeat(jnp.exp(heights), shape[axis_at] // blocks).reshape((-1,) + (1,) * (len(shape) - axis_at - 1))

    gain = one(*pieces[0])
    for cut in pieces[1:]:
        gain = gain * one(*cut)
    return gain


def bell_draw(rng, shape, scale, most, cuts=(), kind=jnp.bfloat16):
    values = scale * jax.random.normal(rng, shape, jnp.float32)
    if cuts:
        values = values * steps_of(rng, shape, cuts, -0.22, 0.18)
    return jnp.clip(values, -most, most).astype(kind)


def setup_inputs(seed: int = 0, part: int = 0) -> dict:
    key_of = jax.random.split(jax.random.key(seed), 7)
    own_keys = jax.random.split(jax.random.fold_in(key_of[6], part), 7)
    return {
        "queries": draw_queries(jax.random.fold_in(jax.random.fold_in(key_of[6], part), 71), part),
        "keys": draw_keys(jax.random.fold_in(jax.random.fold_in(key_of[6], part), 71), part),
        "values": bell_draw(own_keys[2], (SEQ, KV_HEADS * HD), 1.0, 6.0, ((0, 16),)),
        "out_grad": bell_draw(own_keys[3], (SEQ, HEADS * HD), 1.0, 6.0, ((0, 16),)),
        "doc_starts": draw_doc_starts(jax.random.fold_in(jax.random.fold_in(key_of[6], part), 71), part),
        "block_lists": draw_block_lists(jax.random.fold_in(jax.random.fold_in(key_of[6], part), 71), part),
    }


def doc_index(positions, doc_starts):
    return jnp.sum((positions[..., None] >= doc_starts[1:]).astype(jnp.int32), axis=-1)


def reference(queries, keys, values, out_grad, doc_starts, block_lists):
    groups = HEADS // KV_HEADS
    scaling = HD ** -0.5
    key_blocks = keys.reshape(NBLK, BLOCK, KV_HEADS, HD)
    value_blocks = values.reshape(NBLK, BLOCK, KV_HEADS, HD)
    query_blocks = queries.reshape(NBLK, BLOCK, KV_HEADS, groups, HD)
    grad_blocks = out_grad.reshape(NBLK, BLOCK, KV_HEADS, groups, HD)
    offsets = jnp.arange(BLOCK, dtype=jnp.int32)

    def per_block(carried, inputs):
        acc_keys, acc_values = carried
        query_blk, grad_blk, entries, block_index = inputs
        listed = entries >= 0
        clamped = jnp.where(listed, entries, 0).astype(jnp.int32)
        key_tiles = key_blocks[clamped].astype(jnp.float32)
        value_tiles = value_blocks[clamped].astype(jnp.float32)
        query_full = query_blk.astype(jnp.float32)
        grad_full = grad_blk.astype(jnp.float32)
        query_pos = block_index * BLOCK + offsets
        key_pos = clamped[:, None] * BLOCK + offsets[None, :]
        same_doc = doc_index(key_pos, doc_starts)[None] == doc_index(query_pos, doc_starts)[:, None, None]
        causal = key_pos[None] <= query_pos[:, None, None]
        allowed = listed[None, :, None] & causal & same_doc
        scores = jnp.einsum('qgjd,lkgd->gjqlk', query_full, key_tiles) * scaling
        masked = jnp.where(allowed, scores, -1e30)
        row_max = jnp.max(masked, axis=(3, 4), keepdims=True)
        unnormed = jnp.where(allowed, jnp.exp(masked - row_max), 0.0)
        attn_probs = unnormed / jnp.sum(unnormed, axis=(3, 4), keepdims=True)
        probs_low = attn_probs.astype(jnp.bfloat16)
        probs_full = probs_low.astype(jnp.float32)
        attended = jnp.einsum('gjqlk,lkgd->qgjd', probs_full, value_tiles).astype(jnp.bfloat16)
        row_delta = jnp.einsum('qgjd,qgjd->gjq', grad_full, attended.astype(jnp.float32))
        dprobs = jnp.einsum('qgjd,lkgd->gjqlk', grad_full, value_tiles)
        grad_scores = (attn_probs * (dprobs - row_delta[..., None, None])).astype(jnp.bfloat16)
        scores_full = grad_scores.astype(jnp.float32)
        grad_query = (jnp.einsum('gjqlk,lkgd->qgjd', scores_full, key_tiles) * scaling).astype(jnp.bfloat16)
        grad_key_tiles = jnp.einsum('gjqlk,qgjd->lkgd', scores_full, query_full) * scaling
        grad_value_tiles = jnp.einsum('gjqlk,qgjd->lkgd', probs_full, grad_full)
        acc_keys = acc_keys.at[clamped].add(grad_key_tiles)
        acc_values = acc_values.at[clamped].add(grad_value_tiles)
        return (acc_keys, acc_values), (attended, grad_query)

    zeros_acc = jnp.zeros((NBLK, BLOCK, KV_HEADS, HD), jnp.float32)
    indices = jnp.arange(NBLK, dtype=jnp.int32)
    (acc_keys, acc_values), (attended, grad_query) = lax.scan(
        per_block, (zeros_acc, zeros_acc), (query_blocks, grad_blocks, block_lists, indices))
    return (attended.reshape(SEQ, HEADS * HD),
            grad_query.reshape(SEQ, HEADS * HD),
            acc_keys.astype(jnp.bfloat16).reshape(SEQ, KV_HEADS * HD),
            acc_values.astype(jnp.bfloat16).reshape(SEQ, KV_HEADS * HD))
```

```python
import functools

import jax
import jax.numpy as jnp
from jax import lax
from jax.experimental import pallas as pl
from jax.experimental.pallas import tpu as pltpu
from jax.sharding import PartitionSpec as P

HD = 128
HEADS = 16
KV_HEADS = 4
GROUPS = HEADS // KV_HEADS
BLOCK = 128
R_DEV = 2
SCALING = HD ** (-0.5)
LOG2E = 1.4426950408889634
NEG = -1e30


def shifted(value, axis, steps):
    count = lax.axis_size(axis)
    initial, last = (max(0, -steps), min(count, count - steps))
    return lax.ppermute(value, axis, [(source, source + steps) for source in range(initial, last)])


def dot(a, b, dims):
    return lax.dot_general(a, b, (dims, ((), ())), preferred_element_type=jnp.float32)


def attention_kernel(
    lists,
    doc_starts,
    base,
    q_ref,
    g_ref,
    far_ref,
    near_ref,
    own_ref,
    att_ref,
    dq_ref,
    far_out,
    near_out,
    own_out,
    win,
    win_t,
    acc,
    k_sel,
    v_sel,
    kt_sel,
    vt_sel,
    *,
    blocks,
    slots,
    docs,
):
    block = pl.program_id(1)
    rows = blocks * BLOCK

    @pl.when(block == 0)
    def _():
        for part, ref in enumerate((far_ref, near_ref, own_ref)):
            for kind in range(2):
                tile = ref[kind]
                win[kind, part * rows : (part + 1) * rows] = tile
                win_t[kind, :, part * rows : (part + 1) * rows] = tile.T
        acc[...] = jnp.zeros_like(acc)

    first = base[0]
    window_base = first - R_DEV * blocks
    query_pos = (first + block) * BLOCK + lax.broadcasted_iota(jnp.int32, (1, BLOCK), 1)
    start = jnp.zeros((1, BLOCK), jnp.int32)
    for d in range(1, docs):
        start = jnp.where(query_pos >= doc_starts[d], doc_starts[d], start)
    key_iota = lax.broadcasted_iota(jnp.int32, (BLOCK, BLOCK), 0)

    offsets = []
    masks = []
    for s in range(slots):
        entry = lists[block * slots + s]
        listed = entry >= 0
        where = pl.multiple_of(jnp.where(listed, entry - window_base, 0) * BLOCK, BLOCK)
        offsets.append(where)
        span = slice(s * BLOCK, (s + 1) * BLOCK)
        k_sel[span] = win[0, pl.ds(where, BLOCK)]
        v_sel[span] = win[1, pl.ds(where, BLOCK)]
        kt_sel[:, span] = win_t[0, :, pl.ds(where, BLOCK)]
        vt_sel[:, span] = win_t[1, :, pl.ds(where, BLOCK)]
        key_pos = key_iota + jnp.where(listed, entry * BLOCK, -BLOCK)
        allowed = key_pos >= start
        if s == 0:
            allowed = allowed & (key_pos <= query_pos)
        masks.append(allowed)
    allowed = jnp.concatenate(masks, axis=0)
    allowed = jnp.concatenate([allowed] * GROUPS, axis=1)

    def stacked(ref):
        return jnp.concatenate([ref[:, h * HD : (h + 1) * HD] for h in range(GROUPS)], axis=0)

    q4 = stacked(q_ref)
    g4 = stacked(g_ref)
    scores = dot(k_sel[...], q4, ((1,), (1,)))
    scores = jnp.where(allowed, scores, NEG)
    row_max = jnp.max(scores, axis=0, keepdims=True)
    unnormed = jnp.exp2((scores - row_max) * (SCALING * LOG2E))
    total = jnp.sum(unnormed, axis=0, keepdims=True)
    probs = unnormed * (1.0 / total)
    probs_low = probs.astype(jnp.bfloat16)
    att_t = dot(vt_sel[...], probs_low, ((1,), (0,))).astype(jnp.bfloat16)
    g4t = g4.T
    delta = jnp.sum(att_t.astype(jnp.float32) * g4t.astype(jnp.float32), axis=0, keepdims=True)
    att = att_t.T
    dprobs = dot(v_sel[...], g4t, ((1,), (0,)))
    grad_scores = (probs * (dprobs - delta)).astype(jnp.bfloat16)
    dq = (dot(kt_sel[...], grad_scores, ((1,), (0,))) * SCALING).astype(jnp.bfloat16).T
    for h in range(GROUPS):
        att_ref[:, h * HD : (h + 1) * HD] = att[h * BLOCK : (h + 1) * BLOCK]
        dq_ref[:, h * HD : (h + 1) * HD] = dq[h * BLOCK : (h + 1) * BLOCK]
    dk = dot(grad_scores, q4, ((1,), (0,)))
    dv = dot(probs_low, g4, ((1,), (0,)))
    for s in range(slots):
        span = slice(s * BLOCK, (s + 1) * BLOCK)
        at = pl.ds(offsets[s], BLOCK)
        acc[0, at] = acc[0, at] + dk[span]
        acc[1, at] = acc[1, at] + dv[span]

    @pl.when(block == blocks - 1)
    def _():
        for part, ref in enumerate((far_out, near_out, own_out)):
            span = slice(part * rows, (part + 1) * rows)
            ref[0] = (acc[0, span] * SCALING).astype(ref.dtype)
            ref[1] = acc[1, span].astype(ref.dtype)


def attend(lists, doc_starts, base, queries, out_grad, far, near, own):
    blocks, slots = lists.shape
    rows = queries.shape[0]
    width = GROUPS * HD
    window = (R_DEV + 1) * rows
    q_spec = pl.BlockSpec((BLOCK, width), lambda j, b, *_: (b, j))
    kv_spec = pl.BlockSpec((2, rows, HD), lambda j, b, *_: (0, 0, j))
    kernel = functools.partial(
        attention_kernel, blocks=blocks, slots=slots, docs=doc_starts.shape[0]
    )
    return pl.pallas_call(
        kernel,
        grid_spec=pltpu.PrefetchScalarGridSpec(
            num_scalar_prefetch=3,
            grid=(KV_HEADS, blocks),
            in_specs=[q_spec, q_spec, kv_spec, kv_spec, kv_spec],
            out_specs=[q_spec, q_spec, kv_spec, kv_spec, kv_spec],
            scratch_shapes=[
                pltpu.VMEM((2, window, HD), jnp.bfloat16),
                pltpu.VMEM((2, HD, window), jnp.bfloat16),
                pltpu.VMEM((2, window, HD), jnp.float32),
                pltpu.VMEM((slots * BLOCK, HD), jnp.bfloat16),
                pltpu.VMEM((slots * BLOCK, HD), jnp.bfloat16),
                pltpu.VMEM((HD, slots * BLOCK), jnp.bfloat16),
                pltpu.VMEM((HD, slots * BLOCK), jnp.bfloat16),
            ],
        ),
        out_shape=[
            jax.ShapeDtypeStruct(queries.shape, jnp.bfloat16),
            jax.ShapeDtypeStruct(queries.shape, jnp.bfloat16),
            jax.ShapeDtypeStruct(own.shape, jnp.bfloat16),
            jax.ShapeDtypeStruct(own.shape, jnp.bfloat16),
            jax.ShapeDtypeStruct(own.shape, jnp.float32),
        ],
        compiler_params=pltpu.CompilerParams(
            dimension_semantics=("arbitrary", "arbitrary"), vmem_limit_bytes=50 << 20
        ),
        name="attend",
    )(lists.reshape(-1), doc_starts, base, queries, out_grad, far, near, own)


def per_device(queries, keys, values, out_grad, doc_starts, block_lists):
    device = lax.axis_index("ctx")
    blocks = block_lists.shape[0]
    own = jnp.stack([keys, values])
    near = shifted(own, "ctx", 1)
    far = shifted(own, "ctx", 2)
    base = (device * blocks).astype(jnp.int32).reshape(1)
    attended, grad_query, far_part, near_part, own_part = attend(
        block_lists, doc_starts, base, queries, out_grad, far, near, own
    )
    back_far = shifted(far_part, "ctx", -2)
    back_near = shifted(near_part, "ctx", -1)
    summed = own_part + back_near.astype(jnp.float32) + back_far.astype(jnp.float32)
    summed = summed.astype(jnp.bfloat16)
    return attended, grad_query, summed[0], summed[1]


def solution(mesh):
    tokens = P(("grp", "ctx"), None)
    return jax.shard_map(
        per_device,
        mesh=mesh,
        in_specs=(tokens, tokens, tokens, tokens, P("grp"), tokens),
        out_specs=(tokens, tokens, tokens, tokens),
        check_vma=False,
    )
```

```python
import functools

import jax
import jax.numpy as jnp
from jax import lax
from jax.experimental import pallas as pl
from jax.experimental.pallas import tpu as pltpu
from jax.sharding import PartitionSpec as P

HD = 128
HEADS = 16
KV_HEADS = 4
GROUPS = HEADS // KV_HEADS
WIDTH = GROUPS * HD
CORES = 2
PER_CORE = KV_HEADS // CORES
PARTS = 2 * CORES
BLOCK = 128
SCALING = HD ** (-0.5)
LOG2E = 1.4426950408889634
NEG = -1e30
BF16 = jnp.bfloat16
F32 = jnp.float32

ANY = pl.BlockSpec(memory_space=pltpu.HBM)
LARGE = pltpu.CompilerParams(vmem_limit_bytes=60 << 20)
SMALL = pltpu.CompilerParams(vmem_limit_bytes=16 << 20)


def dot(a, b, dims):
    return lax.dot_general(a, b, (dims, ((), ())), preferred_element_type=F32)


def columns(head, width):
    return pl.ds(pl.multiple_of(head * width, width), width)


def pack_kernel(core, keys, values, sib_keys, sib_values, out):
    rows = keys.shape[0]
    for kind, pair in enumerate(((keys, sib_keys), (values, sib_values))):
        for which in range(CORES):
            out[kind, which * rows : (which + 1) * rows] = pair[which][...]


def pack(head, core, keys, values, sib_keys, sib_values):
    rows = keys.shape[0]
    spec = pl.BlockSpec((rows, HD), lambda i, c: (0, c[0] * PER_CORE + head))
    return pl.pallas_call(
        pack_kernel,
        grid_spec=pltpu.PrefetchScalarGridSpec(
            num_scalar_prefetch=1,
            grid=(1,),
            in_specs=[spec] * 4,
            out_specs=pl.BlockSpec((2, CORES * rows, HD), lambda i, c: (0, 0, 0)),
        ),
        out_shape=jax.ShapeDtypeStruct((2, CORES * rows, HD), BF16),
        compiler_params=LARGE,
        name="pack",
    )(core, keys, values, sib_keys, sib_values)


def attention_kernel(*refs, head, blocks, slots, docs, aliased):
    lists, starts, where = refs[:3]
    refs = refs[3:]
    queries, out_grad, sib_queries, sib_out_grad, chip, prev = refs[:6]
    refs = refs[8 if aliased else 6 :]
    att_out, dq_out, returned, chip_part, prev_part = refs[:5]
    (win, win_t, acc, rows_in, rows_out, back, k_sel, v_sel, kt_sel, vt_sel, sems) = refs[5:]
    device = where[0]
    core = lax.rem(device, CORES)
    rows = blocks * BLOCK
    own_columns = columns(core * PER_CORE + head, WIDTH)

    loads = []
    for part, source in enumerate((chip, prev)):
        loads.append((source, win.at[:, part * CORES * rows : (part + 1) * CORES * rows]))
    for i, source in enumerate((queries, out_grad, sib_queries, sib_out_grad)):
        to = rows_in.at[i % 2, pl.ds(i // 2 * rows, rows)]
        loads.append((source.at[:, own_columns], to))
    loads = [pltpu.make_async_copy(a, b, sems.at[i]) for i, (a, b) in enumerate(loads)]
    for copy in loads:
        copy.start()
    acc[...] = jnp.zeros_like(acc)
    for part in range(2):
        loads[part].wait()
        span = slice(part * CORES * rows, (part + 1) * CORES * rows)
        for kind in range(2):
            win_t[kind, :, span] = win[kind, span].T
    loads[2].wait()
    loads[3].wait()

    chip_first = (device - core) * blocks

    def unit(i, is_sibling, live):
        first = (device + is_sibling * (1 - 2 * core)) * blocks
        query_block = first + i
        query_pos = query_block * BLOCK + lax.broadcasted_iota(jnp.int32, (1, BLOCK), 1)
        start = jnp.zeros((1, BLOCK), jnp.int32)
        for d in range(1, docs):
            start = jnp.where(query_pos >= starts[d], starts[d], start)
        key_iota = lax.broadcasted_iota(jnp.int32, (BLOCK, BLOCK), 0)
        offsets = []
        masks = []
        for s in range(live):
            entry = lists[(is_sibling * blocks + i) * slots + s]
            rel = entry - chip_first + CORES * blocks
            owner = lax.rem(lax.div(rel, blocks), CORES)
            part = CORES * (1 - lax.div(rel, CORES * blocks)) + (owner + core) % CORES
            at = pl.multiple_of((part * blocks + lax.rem(rel, blocks)) * BLOCK, BLOCK)
            offsets.append(at)
            span = slice(s * BLOCK, (s + 1) * BLOCK)
            k_sel[span] = win[0, pl.ds(at, BLOCK)]
            v_sel[span] = win[1, pl.ds(at, BLOCK)]
            kt_sel[:, span] = win_t[0, :, pl.ds(at, BLOCK)]
            vt_sel[:, span] = win_t[1, :, pl.ds(at, BLOCK)]
            key_pos = key_iota + entry * BLOCK
            allowed = key_pos >= start
            if s == 0:
                allowed = allowed & (key_pos <= query_pos)
            masks.append(allowed)
        allowed = jnp.concatenate(masks, axis=0)
        allowed = jnp.concatenate([allowed] * GROUPS, axis=1)

        span = slice(0, live * BLOCK)
        at = pl.ds(pl.multiple_of((is_sibling * blocks + i) * BLOCK, BLOCK), BLOCK)

        def stacked(kind):
            tiles = [rows_in[kind, at, h * HD : (h + 1) * HD] for h in range(GROUPS)]
            return jnp.concatenate(tiles, axis=0)

        q4 = stacked(0)
        g4 = stacked(1)
        scores = dot(k_sel[span], q4, ((1,), (1,)))
        scores = jnp.where(allowed, scores, NEG)
        row_max = jnp.max(scores, axis=0, keepdims=True)
        unnormed = jnp.exp2((scores - row_max) * (SCALING * LOG2E))
        total = jnp.sum(unnormed, axis=0, keepdims=True)
        probs = unnormed * (1.0 / total)
        probs_low = probs.astype(BF16)
        att_t = dot(vt_sel[:, span], probs_low, ((1,), (0,))).astype(BF16)
        g4t = g4.T
        delta = jnp.sum(att_t.astype(F32) * g4t.astype(F32), axis=0, keepdims=True)
        att = att_t.T
        dprobs = dot(v_sel[span], g4t, ((1,), (0,)))
        grad_scores = (probs * (dprobs - delta)).astype(BF16)
        dq = (dot(kt_sel[:, span], grad_scores, ((1,), (0,))) * SCALING).astype(BF16).T
        for h in range(GROUPS):
            rows_out[0, at, h * HD : (h + 1) * HD] = att[h * BLOCK : (h + 1) * BLOCK]
            rows_out[1, at, h * HD : (h + 1) * HD] = dq[h * BLOCK : (h + 1) * BLOCK]
        dk = dot(grad_scores, q4, ((1,), (0,)))
        dv = dot(probs_low, g4, ((1,), (0,)))
        for s in range(live):
            span = slice(s * BLOCK, (s + 1) * BLOCK)
            at = pl.ds(offsets[s], BLOCK)
            acc[0, at] = acc[0, at] + dk[span]
            acc[1, at] = acc[1, at] + dv[span]

    def side(is_sibling):
        def step(i, carry):
            base = (is_sibling * blocks + i) * slots
            count = jnp.int32(0)
            for s in range(slots):
                count = count + (lists[base + s] >= 0).astype(jnp.int32)
            for live in range(1, slots + 1):

                @pl.when(count == live)
                def _(live=live):
                    unit(i, is_sibling, live)

            return carry

        return step

    def both(j, carry):
        is_sibling = lax.div(j, blocks)

        @pl.when(j == blocks)
        def _():
            loads[4].wait()
            loads[5].wait()

        return side(is_sibling)(lax.rem(j, blocks), carry)

    lax.fori_loop(0, CORES * blocks, both, 0)

    stores = [
        (rows_out.at[0, :rows], att_out.at[:, own_columns]),
        (rows_out.at[1, :rows], dq_out.at[:, own_columns]),
        (rows_out.at[:, rows:], returned),
        (acc.at[:, : CORES * rows], chip_part),
        (back, prev_part),
    ]
    stores = [pltpu.make_async_copy(a, b, sems.at[i]) for i, (a, b) in enumerate(stores)]
    for copy in stores[:3]:
        copy.start()
    for kind, scale in enumerate((SCALING, 1.0)):
        back[kind] = (acc[kind, CORES * rows :] * scale).astype(BF16)
    for copy in stores[3:]:
        copy.start()
    for copy in stores:
        copy.wait()


def attend(head, lists, starts, where, arrays, full=()):
    slots = lists.shape[1]
    blocks = lists.shape[0] // CORES
    rows = blocks * BLOCK
    window = PARTS * rows
    kernel = functools.partial(
        attention_kernel,
        head=head,
        blocks=blocks,
        slots=slots,
        docs=starts.shape[0],
        aliased=bool(full),
    )
    whole = jax.ShapeDtypeStruct(arrays[0].shape, BF16)
    n_in = len(arrays) + len(full)
    return pl.pallas_call(
        kernel,
        grid_spec=pltpu.PrefetchScalarGridSpec(
            num_scalar_prefetch=3,
            grid=(),
            in_specs=[ANY] * n_in,
            out_specs=[ANY] * 5,
            scratch_shapes=[
                pltpu.VMEM((2, window, HD), BF16),
                pltpu.VMEM((2, HD, window), BF16),
                pltpu.VMEM((2, window, HD), F32),
                pltpu.VMEM((2, CORES * rows, WIDTH), BF16),
                pltpu.VMEM((2, CORES * rows, WIDTH), BF16),
                pltpu.VMEM((2, CORES * rows, HD), BF16),
                pltpu.VMEM((slots * BLOCK, HD), BF16),
                pltpu.VMEM((slots * BLOCK, HD), BF16),
                pltpu.VMEM((HD, slots * BLOCK), BF16),
                pltpu.VMEM((HD, slots * BLOCK), BF16),
                pltpu.SemaphoreType.DMA((8,)),
            ],
        ),
        out_shape=[
            whole,
            whole,
            jax.ShapeDtypeStruct((2, rows, WIDTH), BF16),
            jax.ShapeDtypeStruct((2, CORES * rows, HD), F32),
            jax.ShapeDtypeStruct((2, CORES * rows, HD), BF16),
        ],
        input_output_aliases={9: 0, 10: 1} if full else {},
        compiler_params=LARGE,
        cost_estimate=pl.CostEstimate(
            flops=10 * CORES * blocks * slots * GROUPS * BLOCK * BLOCK * HD,
            transcendentals=CORES * blocks * slots * GROUPS * BLOCK * BLOCK,
            bytes_accessed=10 << 20,
        ),
        name="attend",
    )(lists.reshape(-1), starts, where, *arrays, *full)


def place_kernel(core, *refs):
    h = pl.program_id(0)
    returned, outs = refs[:PER_CORE], refs[-2:]
    for i in range(PER_CORE):

        @pl.when(h == i)
        def _():
            for kind in range(2):
                outs[kind][...] = returned[i][kind]


def place(core, returned, full):
    rows = full[0].shape[0]
    half = rows // 2
    in_spec = pl.BlockSpec((2, half, WIDTH), lambda h, i, *_: (0, i, 0))
    out_spec = pl.BlockSpec((half, WIDTH), lambda h, i, c: (i, (1 - c[0]) * PER_CORE + h))
    return pl.pallas_call(
        place_kernel,
        grid_spec=pltpu.PrefetchScalarGridSpec(
            num_scalar_prefetch=1,
            grid=(PER_CORE, 2),
            in_specs=[in_spec] * PER_CORE + [ANY] * 2,
            out_specs=[out_spec] * 2,
        ),
        out_shape=[jax.ShapeDtypeStruct(f.shape, f.dtype) for f in full],
        input_output_aliases={1 + PER_CORE + i: i for i in range(2)},
        compiler_params=SMALL,
        name="place",
    )(core, *returned, *full)


def total_kernel(chip_part, back, own, other):
    rows = own.shape[1]
    for kind, scale in enumerate((SCALING, 1.0)):
        total = (chip_part[kind] * scale + back[kind].astype(F32)).astype(BF16)
        own[kind] = total[:rows]
        other[kind] = total[rows:]


def total(chip_part, back):
    rows = chip_part.shape[1] // CORES
    return pl.pallas_call(
        total_kernel,
        out_shape=[jax.ShapeDtypeStruct((2, rows, HD), BF16)] * CORES,
        compiler_params=SMALL,
        name="total",
    )(chip_part, back)


def grads_kernel(core, *refs):
    outs = refs[-2:]
    for h in range(PER_CORE):
        for which, owner in enumerate((core[0], 1 - core[0])):
            piece = refs[CORES * h + which]
            at = columns(owner * PER_CORE + h, HD)
            for kind in range(2):
                outs[kind][:, at] = piece[kind]


def grads(core, pieces):
    rows = pieces[0].shape[1]
    strip = pl.BlockSpec((2, rows, HD), lambda i, *_: (0, 0, 0))
    out = pl.BlockSpec((rows, KV_HEADS * HD), lambda i, *_: (0, 0))
    return pl.pallas_call(
        grads_kernel,
        grid_spec=pltpu.PrefetchScalarGridSpec(
            num_scalar_prefetch=1,
            grid=(1,),
            in_specs=[strip] * len(pieces),
            out_specs=[out, out],
        ),
        out_shape=[jax.ShapeDtypeStruct((rows, KV_HEADS * HD), BF16)] * 2,
        compiler_params=SMALL,
        name="grads",
    )(core, *pieces)


def per_device(queries, keys, values, out_grad, doc_starts, block_lists):
    device = lax.axis_index("ctx").astype(jnp.int32)
    count = lax.axis_size("ctx")
    core = lax.rem(device, CORES).reshape(1)
    where = device.reshape(1)
    chips = count // CORES

    pairs = [(2 * c + k, 2 * c + 1 - k) for c in range(chips) for k in range(CORES)]
    same = [(2 * c + k, 2 * c + 2 + k) for c in range(chips - 1) for k in range(CORES)]
    same_back = [(b, a) for a, b in same]

    def send(value, route):
        return lax.ppermute(value, "ctx", route)

    sib_keys, sib_values = send(keys, pairs), send(values, pairs)
    sib_keys, sib_values, late = lax.optimization_barrier(
        (sib_keys, sib_values, (queries, out_grad, block_lists))
    )
    sib_queries, sib_out_grad, sib_lists = [send(value, pairs) for value in late]
    lists = jnp.concatenate([block_lists, sib_lists])
    chip = [pack(h, core, keys, values, sib_keys, sib_values) for h in range(PER_CORE)]
    prev = [send(c, same) for c in chip]

    full, returned, chip_parts, backs = (), [], [], []
    for h in range(PER_CORE):
        arrays = (queries, out_grad, sib_queries, sib_out_grad, chip[h], prev[h])
        *full, to_sibling, chip_part, to_prev = attend(
            h, lists, doc_starts, where, arrays, tuple(full)
        )
        if backs:
            to_prev, to_sibling, backs[-1] = lax.optimization_barrier(
                (to_prev, to_sibling, backs[-1])
            )
        returned.append(send(to_sibling, pairs))
        chip_parts.append(chip_part)
        backs.append(send(to_prev, same_back))
    attended, grad_query = place(core, returned, full)
    attended, grad_query, backs[-1] = lax.optimization_barrier((attended, grad_query, backs[-1]))
    pieces = []
    for chip_part, back in zip(chip_parts, backs):
        own, other = total(chip_part, back)
        pieces += [own, send(other, pairs)]
    return attended, grad_query, *grads(core, pieces)


def solution(mesh):
    tokens = P(("grp", "ctx"), None)
    return jax.shard_map(
        per_device,
        mesh=mesh,
        in_specs=(tokens, tokens, tokens, tokens, P("grp"), tokens),
        out_specs=(tokens, tokens, tokens, tokens),
        check_vma=False,
    )
```

```python
import functools

import jax
import jax.numpy as jnp
from jax import lax
from jax.experimental import pallas as pl
from jax.experimental.pallas import tpu as pltpu
from jax.sharding import PartitionSpec as P

HD = 128
HEADS = 16
KV_HEADS = 4
GROUPS = HEADS // KV_HEADS
WIDTH = GROUPS * HD
CORES = 2
PER_CORE = KV_HEADS // CORES
PARTS = 2 * CORES
BLOCK = 128
SCALING = HD ** (-0.5)
LOG2E = 1.4426950408889634
NEG = -1e30
BF16 = jnp.bfloat16
F32 = jnp.float32

ANY = pl.BlockSpec(memory_space=pltpu.HBM)
VMEM = pl.BlockSpec(memory_space=pltpu.VMEM)
SMALL = pltpu.CompilerParams(vmem_limit_bytes=16 << 20)


def dot(a, b, dims):
    return lax.dot_general(a, b, (dims, ((), ())), preferred_element_type=F32)


def columns(head, width):
    return pl.ds(pl.multiple_of(head * width, width), width)


def pack_kernel(core, keys, values, *outs):
    for h in range(PER_CORE):
        for which, owner in enumerate((core[0], 1 - core[0])):
            at = columns(owner * PER_CORE + h, HD)
            for kind, source in enumerate((keys, values)):
                outs[CORES * h + which][kind] = source[:, at]


def pack(core, keys, values):
    rows = keys.shape[0]
    whole = pl.BlockSpec(keys.shape, lambda i, *_: (0, 0))
    strip = pl.BlockSpec((2, rows, HD), lambda i, *_: (0, 0, 0))
    return pl.pallas_call(
        pack_kernel,
        grid_spec=pltpu.PrefetchScalarGridSpec(
            num_scalar_prefetch=1,
            grid=(1,),
            in_specs=[whole, whole],
            out_specs=[strip] * (CORES * PER_CORE),
        ),
        out_shape=[jax.ShapeDtypeStruct((2, rows, HD), BF16)] * (CORES * PER_CORE),
        compiler_params=SMALL,
        name="pack",
    )(core, *[pltpu.with_memory_space_constraint(a, pltpu.HBM) for a in (keys, values)])


def attention_kernel(*refs, head, blocks, slots, docs, n_prev, n_full):
    lists, starts, where = refs[:3]
    refs = refs[3:]
    row_sources, (own, sib), prev = refs[:4], refs[4:6], refs[6 : 6 + n_prev]
    refs = refs[6 + n_prev + n_full :]
    att_out, dq_out, returned = refs[:3]
    parts_out, scratch = refs[3:-11], refs[-11:]
    win, win_t, acc, rows_in, rows_out, k_sel, v_sel, kt_sel, vt_sel, in_sems, out_sem = scratch
    device = where[0]
    core = lax.rem(device, CORES)
    rows = blocks * BLOCK
    own_columns = columns(core * PER_CORE + head, WIDTH)

    def row_load(kind, j):
        first, second = row_sources[kind], row_sources[2 + kind]
        source = (first if j < blocks else second).at[pl.ds(j % blocks * BLOCK, BLOCK), own_columns]
        to = rows_in.at[kind, j * BLOCK : (j + 1) * BLOCK]
        return pltpu.make_async_copy(source, to, in_sems.at[kind, j])

    for j in range(CORES * blocks):
        for kind in range(2):
            row_load(kind, j).start()
    acc[...] = jnp.zeros_like(acc)
    at = 0
    for source in (own, sib, *prev):
        size = source.shape[1]
        for kind in range(2):
            tile = source[kind]
            win[kind, at : at + size] = tile
            win_t[kind, :, at : at + size] = tile.T
        at += size

    chip_first = (device - core) * blocks

    def unit(i, is_sibling, live):
        first = (device + is_sibling * (1 - 2 * core)) * blocks
        query_block = first + i
        query_pos = query_block * BLOCK + lax.broadcasted_iota(jnp.int32, (1, BLOCK), 1)
        start = jnp.zeros((1, BLOCK), jnp.int32)
        for d in range(1, docs):
            start = jnp.where(query_pos >= starts[d], starts[d], start)
        key_iota = lax.broadcasted_iota(jnp.int32, (BLOCK, BLOCK), 0)
        offsets = []
        masks = []
        for s in range(live):
            entry = lists[(is_sibling * blocks + i) * slots + s]
            rel = entry - chip_first + CORES * blocks
            owner = lax.rem(lax.div(rel, blocks), CORES)
            part = CORES * (1 - lax.div(rel, CORES * blocks)) + (owner + core) % CORES
            at = pl.multiple_of((part * blocks + lax.rem(rel, blocks)) * BLOCK, BLOCK)
            offsets.append(at)
            span = slice(s * BLOCK, (s + 1) * BLOCK)
            k_sel[span] = win[0, pl.ds(at, BLOCK)]
            v_sel[span] = win[1, pl.ds(at, BLOCK)]
            kt_sel[:, span] = win_t[0, :, pl.ds(at, BLOCK)]
            vt_sel[:, span] = win_t[1, :, pl.ds(at, BLOCK)]
            key_pos = key_iota + entry * BLOCK
            allowed = key_pos >= start
            if s == 0:
                allowed = allowed & (key_pos <= query_pos)
            masks.append(allowed)
        allowed = jnp.concatenate(masks, axis=0)
        allowed = jnp.concatenate([allowed] * GROUPS, axis=1)

        span = slice(0, live * BLOCK)
        at = pl.ds(pl.multiple_of((is_sibling * blocks + i) * BLOCK, BLOCK), BLOCK)

        def stacked(kind):
            tiles = [rows_in[kind, at, h * HD : (h + 1) * HD] for h in range(GROUPS)]
            return jnp.concatenate(tiles, axis=0)

        q4 = stacked(0)
        g4 = stacked(1)
        scores = dot(k_sel[span], q4, ((1,), (1,)))
        scores = jnp.where(allowed, scores, NEG)
        row_max = jnp.max(scores, axis=0, keepdims=True)
        unnormed = jnp.exp2((scores - row_max) * (SCALING * LOG2E))
        inverse = 1.0 / jnp.sum(unnormed, axis=0, keepdims=True)
        low = unnormed.astype(BF16)
        att_t = (dot(vt_sel[:, span], low, ((1,), (0,))) * inverse).astype(BF16)
        g4t = g4.T
        g4t_full = g4t.astype(F32)
        delta = jnp.sum(att_t.astype(F32) * g4t_full, axis=0, keepdims=True)
        att = att_t.T
        dprobs = dot(v_sel[span], g4t, ((1,), (0,)))
        grad_scores = (low.astype(F32) * ((dprobs - delta) * inverse)).astype(BF16)
        dq = (dot(kt_sel[:, span], grad_scores, ((1,), (0,))) * SCALING).astype(BF16).T
        g4_scaled = (g4t_full * inverse).astype(BF16).T
        for h in range(GROUPS):
            rows_out[0, at, h * HD : (h + 1) * HD] = att[h * BLOCK : (h + 1) * BLOCK]
            rows_out[1, at, h * HD : (h + 1) * HD] = dq[h * BLOCK : (h + 1) * BLOCK]
        dk = dot(grad_scores, q4, ((1,), (0,)))
        dv = dot(low, g4_scaled, ((1,), (0,)))
        for s in range(live):
            span = slice(s * BLOCK, (s + 1) * BLOCK)
            at = pl.ds(offsets[s], BLOCK)
            acc[0, at] = acc[0, at] + dk[span]
            acc[1, at] = acc[1, at] + dv[span]

    def side(is_sibling):
        def step(i, carry):
            base = (is_sibling * blocks + i) * slots
            count = jnp.int32(0)
            for s in range(slots):
                count = count + (lists[base + s] >= 0).astype(jnp.int32)
            for live in range(1, slots + 1):

                @pl.when(count == live)
                def _(live=live):
                    unit(i, is_sibling, live)

            return carry

        return step

    def both(j, carry):
        is_sibling = lax.div(j, blocks)
        i = lax.rem(j, blocks)
        at = pl.ds(pl.multiple_of(j * BLOCK, BLOCK), BLOCK)
        to = pl.ds(pl.multiple_of(i * BLOCK, BLOCK), BLOCK)
        for kind in range(2):
            landed = rows_in.at[kind, at]
            pltpu.make_async_copy(landed, landed, in_sems.at[kind, j]).wait()
        side(is_sibling)(i, carry)

        @pl.when(j < blocks)
        def _():
            for kind, out in enumerate((att_out, dq_out)):
                done = rows_out.at[kind, at]
                pltpu.make_async_copy(done, out.at[to, own_columns], out_sem).start()

        @pl.when(j >= blocks)
        def _():
            pltpu.make_async_copy(rows_out.at[:, at], returned.at[:, to], out_sem).start()

        return carry

    lax.fori_loop(0, CORES * blocks, both, 0)

    at = 0
    for out in parts_out:
        size = out.shape[1]
        for kind, scale in enumerate((SCALING, 1.0)):
            tile = acc[kind, at : at + size]
            out[kind] = (tile * scale).astype(BF16) if out.dtype == BF16 else tile
        at += size
    pltpu.make_async_copy(rows_out, rows_out, out_sem).wait()


def attend(head, lists, starts, where, arrays, full, parts):
    slots = lists.shape[1]
    blocks = lists.shape[0] // CORES
    rows = blocks * BLOCK
    window = PARTS * rows
    kernel = functools.partial(
        attention_kernel,
        head=head,
        blocks=blocks,
        slots=slots,
        docs=starts.shape[0],
        n_prev=len(arrays) - 6,
        n_full=len(full),
    )
    whole = jax.ShapeDtypeStruct(arrays[0].shape, BF16)
    outs = [jax.ShapeDtypeStruct((2, n * rows, HD), kind) for n, kind in parts]
    return pl.pallas_call(
        kernel,
        grid_spec=pltpu.PrefetchScalarGridSpec(
            num_scalar_prefetch=3,
            grid=(),
            in_specs=[ANY] * 4 + [VMEM] * (len(arrays) - 4) + [ANY] * len(full),
            out_specs=[ANY] * 3 + [VMEM] * len(outs),
            scratch_shapes=[
                pltpu.VMEM((2, window, HD), BF16),
                pltpu.VMEM((2, HD, window), BF16),
                pltpu.VMEM((2, window, HD), F32),
                pltpu.VMEM((2, CORES * rows, WIDTH), BF16),
                pltpu.VMEM((2, CORES * rows, WIDTH), BF16),
                pltpu.VMEM((slots * BLOCK, HD), BF16),
                pltpu.VMEM((slots * BLOCK, HD), BF16),
                pltpu.VMEM((HD, slots * BLOCK), BF16),
                pltpu.VMEM((HD, slots * BLOCK), BF16),
                pltpu.SemaphoreType.DMA((2, CORES * blocks)),
                pltpu.SemaphoreType.DMA,
            ],
        ),
        out_shape=[whole, whole, jax.ShapeDtypeStruct((2, rows, WIDTH), BF16), *outs],
        input_output_aliases={3 + len(arrays) + i: i for i in range(len(full))},
        compiler_params=pltpu.CompilerParams(vmem_limit_bytes=40 << 20),
        cost_estimate=pl.CostEstimate(
            flops=10 * CORES * blocks * slots * GROUPS * BLOCK * BLOCK * HD,
            transcendentals=CORES * blocks * slots * GROUPS * BLOCK * BLOCK,
            bytes_accessed=10 << 20,
        ),
        name="attend",
    )(
        lists.reshape(-1),
        starts,
        where,
        *[pltpu.with_memory_space_constraint(a, pltpu.HBM) for a in arrays[:2]],
        *arrays[2:],
        *full,
    )


def place_kernel(core, *refs):
    h = pl.program_id(0)
    returned, outs = refs[:PER_CORE], refs[-2:]
    for i in range(PER_CORE):

        @pl.when(h == i)
        def _():
            for kind in range(2):
                outs[kind][...] = returned[i][kind]


def place(core, returned, full):
    rows = full[0].shape[0]
    half = rows // 2
    in_spec = pl.BlockSpec((2, half, WIDTH), lambda h, i, *_: (0, i, 0))
    out_spec = pl.BlockSpec((half, WIDTH), lambda h, i, c: (i, (1 - c[0]) * PER_CORE + h))
    return pl.pallas_call(
        place_kernel,
        grid_spec=pltpu.PrefetchScalarGridSpec(
            num_scalar_prefetch=1,
            grid=(PER_CORE, 2),
            in_specs=[in_spec] * PER_CORE + [ANY] * 2,
            out_specs=[out_spec] * 2,
        ),
        out_shape=[jax.ShapeDtypeStruct(f.shape, f.dtype) for f in full],
        input_output_aliases={1 + PER_CORE + i: i for i in range(2)},
        compiler_params=SMALL,
        name="place",
    )(core, *returned, *full)


def total_kernel(chip_part, back, own, other):
    rows = own.shape[1]
    for kind, scale in enumerate((SCALING, 1.0)):
        total = (chip_part[kind] * scale + back[kind].astype(F32)).astype(BF16)
        own[kind] = total[:rows]
        other[kind] = total[rows:]


def total(chip_part, back):
    rows = chip_part.shape[1] // CORES
    return pl.pallas_call(
        total_kernel,
        out_shape=[jax.ShapeDtypeStruct((2, rows, HD), BF16)] * CORES,
        compiler_params=SMALL,
        name="total",
    )(chip_part, back)


def grads_kernel(core, *refs):
    outs = refs[-2:]
    pieces = refs[:-2]
    own_part, own_back, other_part, other_back = pieces[-4:]
    for kind, scale in enumerate((SCALING, 1.0)):
        for which, owner in enumerate((core[0], 1 - core[0])):
            for h in range(PER_CORE - 1):
                at = columns(owner * PER_CORE + h, HD)
                outs[kind][:, at] = pieces[CORES * h + which][kind]
        at = columns(core[0] * PER_CORE + PER_CORE - 1, HD)
        value = own_part[kind] * scale + own_back[kind].astype(F32)
        outs[kind][:, at] = value.astype(BF16)
        at = columns((1 - core[0]) * PER_CORE + PER_CORE - 1, HD)
        value = other_part[kind].astype(F32) + other_back[kind].astype(F32)
        outs[kind][:, at] = value.astype(BF16)


def grads(core, pieces):
    rows = pieces[0].shape[1]
    strip = pl.BlockSpec((2, rows, HD), lambda i, *_: (0, 0, 0))
    out = pl.BlockSpec((rows, KV_HEADS * HD), lambda i, *_: (0, 0))
    return pl.pallas_call(
        grads_kernel,
        grid_spec=pltpu.PrefetchScalarGridSpec(
            num_scalar_prefetch=1,
            grid=(1,),
            in_specs=[strip] * len(pieces),
            out_specs=[out, out],
        ),
        out_shape=[jax.ShapeDtypeStruct((rows, KV_HEADS * HD), BF16)] * 2,
        compiler_params=SMALL,
        name="grads",
    )(core, *pieces)


def per_device(queries, keys, values, out_grad, doc_starts, block_lists):
    device = lax.axis_index("ctx").astype(jnp.int32)
    count = lax.axis_size("ctx")
    core = lax.rem(device, CORES).reshape(1)
    where = device.reshape(1)
    chips = count // CORES

    pairs = [(2 * c + k, 2 * c + 1 - k) for c in range(chips) for k in range(CORES)]
    same = [(2 * c + k, 2 * c + 2 + k) for c in range(chips - 1) for k in range(CORES)]
    cross = [(2 * c + k, 2 * c + 3 - k) for c in range(chips - 1) for k in range(CORES)]
    same_back = [(b, a) for a, b in same]
    cross_back = [(b, a) for a, b in cross]

    def send(value, route):
        return lax.ppermute(value, "ctx", route)

    packed = pack(core, keys, values)
    own, other, sib, prev = packed[0::CORES], packed[1::CORES], [], []
    for h in range(PER_CORE):
        mine, theirs = own[h], other[h]
        sib.append(send(theirs, pairs))
        if h == 0:
            prev.append([send(mine, same), send(theirs, cross)])
        else:
            prev.append([send(jnp.concatenate([mine, sib[h]], axis=1), same)])
    sib_queries, sib_out_grad = send(queries, pairs), send(out_grad, pairs)
    lists = jnp.concatenate([block_lists, send(block_lists, pairs)])

    full, returned, pieces, back = (), [], [], None
    for h in range(PER_CORE):
        last = h == PER_CORE - 1
        parts = [(1, F32)] + [(1, BF16)] * 3 if last else [(CORES, F32), (CORES, BF16)]
        arrays = (queries, out_grad, sib_queries, sib_out_grad, own[h], sib[h], *prev[h])
        att, dq, to_sibling, *parts = attend(h, lists, doc_starts, where, arrays, full, parts)
        full = (att, dq)
        if h > 0:
            to_sibling, parts, back = lax.optimization_barrier((to_sibling, parts, back))
            own_total, other_total = total(chip_part, back)
            pieces += [own_total, send(other_total, pairs)]
        returned.append(send(to_sibling, pairs))
        if not last:
            chip_part, to_prev = parts
            back = send(to_prev, same_back)
        else:
            own_part, sib_part, to_same, to_cross = parts
            own_back, other_back = send(to_same, same_back), send(to_cross, cross_back)
            other_part = send(sib_part, pairs)
    attended, grad_query = place(core, returned, full)
    attended, grad_query, other_back = lax.optimization_barrier((attended, grad_query, other_back))
    pieces += [own_part, own_back, other_part, other_back]
    return attended, grad_query, *grads(core, pieces)


def solution(mesh):
    tokens = P(("grp", "ctx"), None)
    return jax.shard_map(
        per_device,
        mesh=mesh,
        in_specs=(tokens, tokens, tokens, tokens, P("grp"), tokens),
        out_specs=(tokens, tokens, tokens, tokens),
        check_vma=False,
    )
```

```python
import functools

import jax
import jax.numpy as jnp
from jax import lax
from jax.experimental import pallas as pl
from jax.experimental.pallas import tpu as pltpu
from jax.sharding import PartitionSpec as P

HD = 128
HEADS = 16
KV_HEADS = 4
GROUPS = HEADS // KV_HEADS
WIDTH = GROUPS * HD
CORES = 2
PER_CORE = KV_HEADS // CORES
PARTS = 2 * CORES
BLOCK = 128
SCALING = HD ** (-0.5)
LOG2E = 1.4426950408889634
NEG = -1e30
BF16 = jnp.bfloat16
F32 = jnp.float32

ANY = pl.BlockSpec(memory_space=pltpu.HBM)
VMEM = pl.BlockSpec(memory_space=pltpu.VMEM)
SMALL = pltpu.CompilerParams(vmem_limit_bytes=16 << 20)


def dot(a, b, dims):
    return lax.dot_general(a, b, (dims, ((), ())), preferred_element_type=F32)


def columns(head, width):
    return pl.ds(pl.multiple_of(head * width, width), width)


def pack_kernel(core, keys, values, *outs):
    for h in range(PER_CORE):
        for which, owner in enumerate((core[0], 1 - core[0])):
            at = columns(owner * PER_CORE + h, HD)
            for kind, source in enumerate((keys, values)):
                outs[CORES * h + which][kind] = source[:, at]


def pack(core, keys, values):
    rows = keys.shape[0]
    whole = pl.BlockSpec(keys.shape, lambda i, *_: (0, 0))
    strip = pl.BlockSpec((2, rows, HD), lambda i, *_: (0, 0, 0))
    return pl.pallas_call(
        pack_kernel,
        grid_spec=pltpu.PrefetchScalarGridSpec(
            num_scalar_prefetch=1,
            grid=(1,),
            in_specs=[whole, whole],
            out_specs=[strip] * (CORES * PER_CORE),
        ),
        out_shape=[jax.ShapeDtypeStruct((2, rows, HD), BF16)] * (CORES * PER_CORE),
        compiler_params=SMALL,
        name="pack",
    )(core, *[pltpu.with_memory_space_constraint(a, pltpu.HBM) for a in (keys, values)])


def attention_kernel(*refs, head, blocks, slots, docs, n_prev, n_full):
    lists, starts, where = refs[:3]
    refs = refs[3:]
    row_sources, (own, sib), prev = refs[:4], refs[4:6], refs[6 : 6 + n_prev]
    refs = refs[6 + n_prev + n_full :]
    att_out, dq_out, returned = refs[:3]
    parts_out, scratch = refs[3:-11], refs[-11:]
    win, win_t, acc, rows_in, rows_out, k_sel, v_sel, kt_sel, vt_sel, in_sems, out_sem = scratch
    device = where[0]
    core = lax.rem(device, CORES)
    rows = blocks * BLOCK
    own_columns = columns(core * PER_CORE + head, WIDTH)

    def row_load(kind, j):
        first, second = row_sources[kind], row_sources[2 + kind]
        source = (first if j < blocks else second).at[pl.ds(j % blocks * BLOCK, BLOCK), own_columns]
        to = rows_in.at[kind, j * BLOCK : (j + 1) * BLOCK]
        return pltpu.make_async_copy(source, to, in_sems.at[kind, j])

    for j in range(CORES * blocks):
        for kind in range(2):
            row_load(kind, j).start()
    acc[...] = jnp.zeros_like(acc)
    at = 0
    for source in (own, sib, *prev):
        size = source.shape[1]
        for kind in range(2):
            tile = source[kind]
            win[kind, at : at + size] = tile
            win_t[kind, :, at : at + size] = tile.T
        at += size

    chip_first = (device - core) * blocks

    def unit(i, is_sibling, live):
        first = (device + is_sibling * (1 - 2 * core)) * blocks
        query_block = first + i
        query_pos = query_block * BLOCK + lax.broadcasted_iota(jnp.int32, (1, BLOCK), 1)
        start = jnp.zeros((1, BLOCK), jnp.int32)
        for d in range(1, docs):
            start = jnp.where(query_pos >= starts[d], starts[d], start)
        key_iota = lax.broadcasted_iota(jnp.int32, (BLOCK, BLOCK), 0)
        offsets = []
        masks = []
        for s in range(live):
            entry = lists[(is_sibling * blocks + i) * slots + s]
            rel = entry - chip_first + CORES * blocks
            owner = lax.rem(lax.div(rel, blocks), CORES)
            part = CORES * (1 - lax.div(rel, CORES * blocks)) + (owner + core) % CORES
            at = pl.multiple_of((part * blocks + lax.rem(rel, blocks)) * BLOCK, BLOCK)
            offsets.append(at)
            span = slice(s * BLOCK, (s + 1) * BLOCK)
            k_sel[span] = win[0, pl.ds(at, BLOCK)]
            v_sel[span] = win[1, pl.ds(at, BLOCK)]
            kt_sel[:, span] = win_t[0, :, pl.ds(at, BLOCK)]
            vt_sel[:, span] = win_t[1, :, pl.ds(at, BLOCK)]
            key_pos = key_iota + entry * BLOCK
            allowed = key_pos >= start
            if s == 0:
                allowed = allowed & (key_pos <= query_pos)
            masks.append(allowed)
        allowed = jnp.concatenate(masks, axis=0)
        allowed = jnp.concatenate([allowed] * GROUPS, axis=1)

        span = slice(0, live * BLOCK)
        at = pl.ds(pl.multiple_of((is_sibling * blocks + i) * BLOCK, BLOCK), BLOCK)

        def stacked(kind):
            tiles = [rows_in[kind, at, h * HD : (h + 1) * HD] for h in range(GROUPS)]
            return jnp.concatenate(tiles, axis=0)

        q4 = stacked(0)
        g4 = stacked(1)
        scores = dot(k_sel[span], q4, ((1,), (1,)))
        scores = jnp.where(allowed, scores, NEG)
        row_max = jnp.max(scores, axis=0, keepdims=True)
        unnormed = jnp.exp2((scores - row_max) * (SCALING * LOG2E))
        inverse = 1.0 / jnp.sum(unnormed, axis=0, keepdims=True)
        low = unnormed.astype(BF16)
        att_t = (dot(vt_sel[:, span], low, ((1,), (0,))) * inverse).astype(BF16)
        g4t = g4.T
        g4t_full = g4t.astype(F32)
        delta = jnp.sum(att_t.astype(F32) * g4t_full, axis=0, keepdims=True)
        att = att_t.T
        dprobs = dot(v_sel[span], g4t, ((1,), (0,)))
        grad_scores = (low.astype(F32) * ((dprobs - delta) * inverse)).astype(BF16)
        dq = (dot(kt_sel[:, span], grad_scores, ((1,), (0,))) * SCALING).astype(BF16).T
        g4_scaled = (g4t_full * inverse).astype(BF16).T
        for h in range(GROUPS):
            rows_out[0, at, h * HD : (h + 1) * HD] = att[h * BLOCK : (h + 1) * BLOCK]
            rows_out[1, at, h * HD : (h + 1) * HD] = dq[h * BLOCK : (h + 1) * BLOCK]
        dk = dot(grad_scores, q4, ((1,), (0,)))
        dv = dot(low, g4_scaled, ((1,), (0,)))
        for s in range(live):
            span = slice(s * BLOCK, (s + 1) * BLOCK)
            at = pl.ds(offsets[s], BLOCK)
            acc[0, at] = acc[0, at] + dk[span]
            acc[1, at] = acc[1, at] + dv[span]

    def side(is_sibling):
        def step(i, carry):
            base = (is_sibling * blocks + i) * slots
            count = jnp.int32(0)
            for s in range(slots):
                count = count + (lists[base + s] >= 0).astype(jnp.int32)
            for live in range(1, slots + 1):

                @pl.when(count == live)
                def _(live=live):
                    unit(i, is_sibling, live)

            return carry

        return step

    def both(j, carry):
        is_sibling = lax.div(j, blocks)
        i = lax.rem(j, blocks)
        at = pl.ds(pl.multiple_of(j * BLOCK, BLOCK), BLOCK)
        to = pl.ds(pl.multiple_of(i * BLOCK, BLOCK), BLOCK)
        for kind in range(2):
            landed = rows_in.at[kind, at]
            pltpu.make_async_copy(landed, landed, in_sems.at[kind, j]).wait()
        side(is_sibling)(i, carry)

        @pl.when(j < blocks)
        def _():
            for kind, out in enumerate((att_out, dq_out)):
                done = rows_out.at[kind, at]
                pltpu.make_async_copy(done, out.at[to, own_columns], out_sem).start()

        @pl.when(j >= blocks)
        def _():
            pltpu.make_async_copy(rows_out.at[:, at], returned.at[:, to], out_sem).start()

        return carry

    lax.fori_loop(0, CORES * blocks, both, 0)

    at = 0
    for out in parts_out:
        size = out.shape[1]
        for kind, scale in enumerate((SCALING, 1.0)):
            tile = acc[kind, at : at + size]
            out[kind] = (tile * scale).astype(BF16) if out.dtype == BF16 else tile
        at += size
    pltpu.make_async_copy(rows_out, rows_out, out_sem).wait()


def attend(head, lists, starts, where, arrays, full, parts):
    slots = lists.shape[1]
    blocks = lists.shape[0] // CORES
    rows = blocks * BLOCK
    window = PARTS * rows
    kernel = functools.partial(
        attention_kernel,
        head=head,
        blocks=blocks,
        slots=slots,
        docs=starts.shape[0],
        n_prev=len(arrays) - 6,
        n_full=len(full),
    )
    whole = jax.ShapeDtypeStruct(arrays[0].shape, BF16)
    outs = [jax.ShapeDtypeStruct((2, n * rows, HD), kind) for n, kind in parts]
    return pl.pallas_call(
        kernel,
        grid_spec=pltpu.PrefetchScalarGridSpec(
            num_scalar_prefetch=3,
            grid=(),
            in_specs=[ANY] * 4 + [VMEM] * (len(arrays) - 4) + [ANY] * len(full),
            out_specs=[ANY] * 3 + [VMEM] * len(outs),
            scratch_shapes=[
                pltpu.VMEM((2, window, HD), BF16),
                pltpu.VMEM((2, HD, window), BF16),
                pltpu.VMEM((2, window, HD), F32),
                pltpu.VMEM((2, CORES * rows, WIDTH), BF16),
                pltpu.VMEM((2, CORES * rows, WIDTH), BF16),
                pltpu.VMEM((slots * BLOCK, HD), BF16),
                pltpu.VMEM((slots * BLOCK, HD), BF16),
                pltpu.VMEM((HD, slots * BLOCK), BF16),
                pltpu.VMEM((HD, slots * BLOCK), BF16),
                pltpu.SemaphoreType.DMA((2, CORES * blocks)),
                pltpu.SemaphoreType.DMA,
            ],
        ),
        out_shape=[whole, whole, jax.ShapeDtypeStruct((2, rows, WIDTH), BF16), *outs],
        input_output_aliases={3 + len(arrays) + i: i for i in range(len(full))},
        compiler_params=pltpu.CompilerParams(vmem_limit_bytes=40 << 20),
        cost_estimate=pl.CostEstimate(
            flops=10 * CORES * blocks * slots * GROUPS * BLOCK * BLOCK * HD,
            transcendentals=CORES * blocks * slots * GROUPS * BLOCK * BLOCK,
            bytes_accessed=10 << 20,
        ),
        name="attend",
    )(
        lists.reshape(-1),
        starts,
        where,
        *[pltpu.with_memory_space_constraint(a, pltpu.HBM) for a in arrays[:2]],
        *arrays[2:],
        *full,
    )


def place_kernel(core, *refs):
    h = pl.program_id(0)
    returned, outs = refs[:PER_CORE], refs[-2:]
    for i in range(PER_CORE):

        @pl.when(h == i)
        def _():
            for kind in range(2):
                outs[kind][...] = returned[i][kind]


def place(core, returned, full):
    rows = full[0].shape[0]
    half = rows // 2
    in_spec = pl.BlockSpec((2, half, WIDTH), lambda h, i, *_: (0, i, 0))
    out_spec = pl.BlockSpec((half, WIDTH), lambda h, i, c: (i, (1 - c[0]) * PER_CORE + h))
    return pl.pallas_call(
        place_kernel,
        grid_spec=pltpu.PrefetchScalarGridSpec(
            num_scalar_prefetch=1,
            grid=(PER_CORE, 2),
            in_specs=[in_spec] * PER_CORE + [ANY] * 2,
            out_specs=[out_spec] * 2,
        ),
        out_shape=[jax.ShapeDtypeStruct(f.shape, f.dtype) for f in full],
        input_output_aliases={1 + PER_CORE + i: i for i in range(2)},
        compiler_params=SMALL,
        name="place",
    )(core, *returned, *full)


def total_kernel(chip_part, back, own, other):
    rows = own.shape[1]
    for kind, scale in enumerate((SCALING, 1.0)):
        total = (chip_part[kind] * scale + back[kind].astype(F32)).astype(BF16)
        own[kind] = total[:rows]
        other[kind] = total[rows:]


def total(chip_part, back):
    rows = chip_part.shape[1] // CORES
    return pl.pallas_call(
        total_kernel,
        out_shape=[jax.ShapeDtypeStruct((2, rows, HD), BF16)] * CORES,
        compiler_params=SMALL,
        name="total",
    )(chip_part, back)


def grads_kernel(core, *refs):
    outs = refs[-2:]
    pieces = refs[:-2]
    own_part, own_back, other_part, other_back = pieces[-4:]
    for kind, scale in enumerate((SCALING, 1.0)):
        for which, owner in enumerate((core[0], 1 - core[0])):
            for h in range(PER_CORE - 1):
                at = columns(owner * PER_CORE + h, HD)
                outs[kind][:, at] = pieces[CORES * h + which][kind]
        at = columns(core[0] * PER_CORE + PER_CORE - 1, HD)
        value = own_part[kind] * scale + own_back[kind].astype(F32)
        outs[kind][:, at] = value.astype(BF16)
        at = columns((1 - core[0]) * PER_CORE + PER_CORE - 1, HD)
        value = other_part[kind].astype(F32) + other_back[kind].astype(F32)
        outs[kind][:, at] = value.astype(BF16)


def grads(core, pieces):
    rows = pieces[0].shape[1]
    strip = pl.BlockSpec((2, rows, HD), lambda i, *_: (0, 0, 0))
    out = pl.BlockSpec((rows, KV_HEADS * HD), lambda i, *_: (0, 0))
    return pl.pallas_call(
        grads_kernel,
        grid_spec=pltpu.PrefetchScalarGridSpec(
            num_scalar_prefetch=1,
            grid=(1,),
            in_specs=[strip] * len(pieces),
            out_specs=[out, out],
        ),
        out_shape=[jax.ShapeDtypeStruct((rows, KV_HEADS * HD), BF16)] * 2,
        compiler_params=SMALL,
        name="grads",
    )(core, *pieces)


def per_device(queries, keys, values, out_grad, doc_starts, block_lists):
    device = lax.axis_index("ctx").astype(jnp.int32)
    count = lax.axis_size("ctx")
    core = lax.rem(device, CORES).reshape(1)
    where = device.reshape(1)
    chips = count // CORES

    pairs = [(2 * c + k, 2 * c + 1 - k) for c in range(chips) for k in range(CORES)]
    same = [(2 * c + k, 2 * c + 2 + k) for c in range(chips - 1) for k in range(CORES)]
    cross = [(2 * c + k, 2 * c + 3 - k) for c in range(chips - 1) for k in range(CORES)]
    same_back = [(b, a) for a, b in same]
    cross_back = [(b, a) for a, b in cross]

    def send(value, route):
        return lax.ppermute(value, "ctx", route)

    packed = pack(core, keys, values)
    own, other, sib, prev = packed[0::CORES], packed[1::CORES], [], []
    for h in range(PER_CORE):
        mine, theirs = own[h], other[h]
        sib.append(send(theirs, pairs))
        if h == 0:
            prev.append([send(mine, same), send(theirs, cross)])
        else:
            prev.append([send(jnp.concatenate([mine, sib[h]], axis=1), same)])
    late, _ = lax.optimization_barrier(((queries, out_grad, block_lists), packed))
    sib_queries, sib_out_grad, sib_lists = [send(value, pairs) for value in late]
    lists = jnp.concatenate([block_lists, sib_lists])

    full, returned, pieces, back = (), [], [], None
    for h in range(PER_CORE):
        last = h == PER_CORE - 1
        parts = [(1, F32)] + [(1, BF16)] * 3 if last else [(CORES, F32), (CORES, BF16)]
        arrays = (queries, out_grad, sib_queries, sib_out_grad, own[h], sib[h], *prev[h])
        att, dq, to_sibling, *parts = attend(h, lists, doc_starts, where, arrays, full, parts)
        full = (att, dq)
        if h > 0:
            to_sibling, parts, back = lax.optimization_barrier((to_sibling, parts, back))
            own_total, other_total = total(chip_part, back)
            pieces += [own_total, send(other_total, pairs)]
        returned.append(send(to_sibling, pairs))
        if not last:
            chip_part, to_prev = parts
            back = send(to_prev, same_back)
        else:
            own_part, sib_part, to_same, to_cross = parts
            own_back, other_back = send(to_same, same_back), send(to_cross, cross_back)
            other_part = send(sib_part, pairs)
    attended, grad_query = place(core, returned, full)
    attended, grad_query, other_back = lax.optimization_barrier((attended, grad_query, other_back))
    pieces += [own_part, own_back, other_part, other_back]
    return attended, grad_query, *grads(core, pieces)


def solution(mesh):
    tokens = P(("grp", "ctx"), None)
    return jax.shard_map(
        per_device,
        mesh=mesh,
        in_specs=(tokens, tokens, tokens, tokens, P("grp"), tokens),
        out_specs=(tokens, tokens, tokens, tokens),
        check_vma=False,
    )
```

```python
import functools

import jax
import jax.numpy as jnp
from jax import lax
from jax.experimental import pallas as pl
from jax.experimental.pallas import tpu as pltpu
from jax.sharding import PartitionSpec as P

HD = 128
HEADS = 16
KV_HEADS = 4
GROUPS = HEADS // KV_HEADS
WIDTH = GROUPS * HD
CORES = 2
PER_CORE = KV_HEADS // CORES
PARTS = 2 * CORES
BLOCK = 128
SCALING = HD ** (-0.5)
LOG2E = 1.4426950408889634
NEG = -1e30
BF16 = jnp.bfloat16
F32 = jnp.float32

ANY = pl.BlockSpec(memory_space=pltpu.HBM)
VMEM = pl.BlockSpec(memory_space=pltpu.VMEM)
SMALL = pltpu.CompilerParams(vmem_limit_bytes=16 << 20)


def dot(a, b, dims):
    return lax.dot_general(a, b, (dims, ((), ())), preferred_element_type=F32)


def columns(head, width):
    return pl.ds(pl.multiple_of(head * width, width), width)


def pack_kernel(core, keys, values, *outs):
    for h in range(PER_CORE):
        for which, owner in enumerate((core[0], 1 - core[0])):
            at = columns(owner * PER_CORE + h, HD)
            for kind, source in enumerate((keys, values)):
                outs[CORES * h + which][kind] = source[:, at]


def pack(core, keys, values):
    rows = keys.shape[0]
    whole = pl.BlockSpec(keys.shape, lambda i, *_: (0, 0))
    strip = pl.BlockSpec((2, rows, HD), lambda i, *_: (0, 0, 0))
    return pl.pallas_call(
        pack_kernel,
        grid_spec=pltpu.PrefetchScalarGridSpec(
            num_scalar_prefetch=1,
            grid=(1,),
            in_specs=[whole, whole],
            out_specs=[strip] * (CORES * PER_CORE),
        ),
        out_shape=[jax.ShapeDtypeStruct((2, rows, HD), BF16)] * (CORES * PER_CORE),
        compiler_params=SMALL,
        name="pack",
    )(core, *[pltpu.with_memory_space_constraint(a, pltpu.HBM) for a in (keys, values)])


def attention_kernel(*refs, head, blocks, slots, docs, n_prev, n_full):
    lists, starts, where = refs[:3]
    refs = refs[3:]
    row_sources, (own, sib), prev = refs[:4], refs[4:6], refs[6 : 6 + n_prev]
    refs = refs[6 + n_prev + n_full :]
    att_out, dq_out, returned = refs[:3]
    parts_out, scratch = refs[3:-11], refs[-11:]
    win, win_t, acc, rows_in, rows_out, k_sel, v_sel, kt_sel, vt_sel, in_sems, out_sem = scratch
    device = where[0]
    core = lax.rem(device, CORES)
    rows = blocks * BLOCK
    own_columns = columns(core * PER_CORE + head, WIDTH)

    def row_load(kind, j):
        first, second = row_sources[kind], row_sources[2 + kind]
        source = (first if j < blocks else second).at[pl.ds(j % blocks * BLOCK, BLOCK), own_columns]
        to = rows_in.at[kind, j * BLOCK : (j + 1) * BLOCK]
        return pltpu.make_async_copy(source, to, in_sems.at[kind, j])

    for j in range(CORES * blocks):
        for kind in range(2):
            row_load(kind, j).start()
    acc[...] = jnp.zeros_like(acc)
    at = 0
    for source in (own, sib, *prev):
        size = source.shape[1]
        for kind in range(2):
            tile = source[kind]
            win[kind, at : at + size] = tile
            win_t[kind, :, at : at + size] = tile.T
        at += size

    chip_first = (device - core) * blocks

    def unit(i, is_sibling, live):
        first = (device + is_sibling * (1 - 2 * core)) * blocks
        query_block = first + i
        query_pos = query_block * BLOCK + lax.broadcasted_iota(jnp.int32, (1, BLOCK), 1)
        start = jnp.zeros((1, BLOCK), jnp.int32)
        for d in range(1, docs):
            start = jnp.where(query_pos >= starts[d], starts[d], start)
        key_iota = lax.broadcasted_iota(jnp.int32, (BLOCK, BLOCK), 0)
        offsets = []
        masks = []
        for s in range(live):
            entry = lists[(is_sibling * blocks + i) * slots + s]
            rel = entry - chip_first + CORES * blocks
            owner = lax.rem(lax.div(rel, blocks), CORES)
            part = CORES * (1 - lax.div(rel, CORES * blocks)) + (owner + core) % CORES
            at = pl.multiple_of((part * blocks + lax.rem(rel, blocks)) * BLOCK, BLOCK)
            offsets.append(at)
            span = slice(s * BLOCK, (s + 1) * BLOCK)
            k_sel[span] = win[0, pl.ds(at, BLOCK)]
            v_sel[span] = win[1, pl.ds(at, BLOCK)]
            kt_sel[:, span] = win_t[0, :, pl.ds(at, BLOCK)]
            vt_sel[:, span] = win_t[1, :, pl.ds(at, BLOCK)]
            key_pos = key_iota + entry * BLOCK
            allowed = key_pos >= start
            if s == 0:
                allowed = allowed & (key_pos <= query_pos)
            masks.append(allowed)
        allowed = jnp.concatenate(masks, axis=0)
        allowed = jnp.concatenate([allowed] * GROUPS, axis=1)

        span = slice(0, live * BLOCK)
        at = pl.ds(pl.multiple_of((is_sibling * blocks + i) * BLOCK, BLOCK), BLOCK)

        def stacked(kind):
            tiles = [rows_in[kind, at, h * HD : (h + 1) * HD] for h in range(GROUPS)]
            return jnp.concatenate(tiles, axis=0)

        q4 = stacked(0)
        g4 = stacked(1)
        scores = dot(k_sel[span], q4, ((1,), (1,)))
        scores = jnp.where(allowed, scores, NEG)
        row_max = jnp.max(scores, axis=0, keepdims=True)
        unnormed = jnp.exp2((scores - row_max) * (SCALING * LOG2E))
        inverse = 1.0 / jnp.sum(unnormed, axis=0, keepdims=True)
        low = unnormed.astype(BF16)
        att_t = (dot(vt_sel[:, span], low, ((1,), (0,))) * inverse).astype(BF16)
        g4t = g4.T
        g4t_full = g4t.astype(F32)
        delta = jnp.sum(att_t.astype(F32) * g4t_full, axis=0, keepdims=True)
        att = att_t.T
        dprobs = dot(v_sel[span], g4t, ((1,), (0,)))
        grad_scores = (low.astype(F32) * ((dprobs - delta) * inverse)).astype(BF16)
        dq = (dot(kt_sel[:, span], grad_scores, ((1,), (0,))) * SCALING).astype(BF16).T
        g4_scaled = (g4t_full * inverse).astype(BF16).T
        for h in range(GROUPS):
            rows_out[0, at, h * HD : (h + 1) * HD] = att[h * BLOCK : (h + 1) * BLOCK]
            rows_out[1, at, h * HD : (h + 1) * HD] = dq[h * BLOCK : (h + 1) * BLOCK]
        dk = dot(grad_scores, q4, ((1,), (0,)))
        dv = dot(low, g4_scaled, ((1,), (0,)))
        for s in range(live):
            span = slice(s * BLOCK, (s + 1) * BLOCK)
            at = pl.ds(offsets[s], BLOCK)
            acc[0, at] = acc[0, at] + dk[span]
            acc[1, at] = acc[1, at] + dv[span]

    def side(is_sibling):
        def step(i, carry):
            base = (is_sibling * blocks + i) * slots
            count = jnp.int32(0)
            for s in range(slots):
                count = count + (lists[base + s] >= 0).astype(jnp.int32)
            for live in range(1, slots + 1):

                @pl.when(count == live)
                def _(live=live):
                    unit(i, is_sibling, live)

            return carry

        return step

    def both(j, carry):
        is_sibling = lax.div(j, blocks)
        i = lax.rem(j, blocks)
        at = pl.ds(pl.multiple_of(j * BLOCK, BLOCK), BLOCK)
        to = pl.ds(pl.multiple_of(i * BLOCK, BLOCK), BLOCK)
        for kind in range(2):
            landed = rows_in.at[kind, at]
            pltpu.make_async_copy(landed, landed, in_sems.at[kind, j]).wait()
        side(is_sibling)(i, carry)

        @pl.when(j < blocks)
        def _():
            for kind, out in enumerate((att_out, dq_out)):
                done = rows_out.at[kind, at]
                pltpu.make_async_copy(done, out.at[to, own_columns], out_sem).start()

        @pl.when(j >= blocks)
        def _():
            pltpu.make_async_copy(rows_out.at[:, at], returned.at[:, to], out_sem).start()

        return carry

    lax.fori_loop(0, CORES * blocks, both, 0)

    at = 0
    for out in parts_out:
        size = out.shape[1]
        for kind, scale in enumerate((SCALING, 1.0)):
            tile = acc[kind, at : at + size]
            out[kind] = (tile * scale).astype(BF16) if out.dtype == BF16 else tile
        at += size
    pltpu.make_async_copy(rows_out, rows_out, out_sem).wait()


def attend(head, lists, starts, where, arrays, full, parts):
    slots = lists.shape[1]
    blocks = lists.shape[0] // CORES
    rows = blocks * BLOCK
    window = PARTS * rows
    kernel = functools.partial(
        attention_kernel,
        head=head,
        blocks=blocks,
        slots=slots,
        docs=starts.shape[0],
        n_prev=len(arrays) - 6,
        n_full=len(full),
    )
    whole = jax.ShapeDtypeStruct(arrays[0].shape, BF16)
    outs = [jax.ShapeDtypeStruct((2, n * rows, HD), kind) for n, kind in parts]
    return pl.pallas_call(
        kernel,
        grid_spec=pltpu.PrefetchScalarGridSpec(
            num_scalar_prefetch=3,
            grid=(),
            in_specs=[ANY] * 4 + [VMEM] * (len(arrays) - 4) + [ANY] * len(full),
            out_specs=[ANY] * 3 + [VMEM] * len(outs),
            scratch_shapes=[
                pltpu.VMEM((2, window, HD), BF16),
                pltpu.VMEM((2, HD, window), BF16),
                pltpu.VMEM((2, window, HD), F32),
                pltpu.VMEM((2, CORES * rows, WIDTH), BF16),
                pltpu.VMEM((2, CORES * rows, WIDTH), BF16),
                pltpu.VMEM((slots * BLOCK, HD), BF16),
                pltpu.VMEM((slots * BLOCK, HD), BF16),
                pltpu.VMEM((HD, slots * BLOCK), BF16),
                pltpu.VMEM((HD, slots * BLOCK), BF16),
                pltpu.SemaphoreType.DMA((2, CORES * blocks)),
                pltpu.SemaphoreType.DMA,
            ],
        ),
        out_shape=[whole, whole, jax.ShapeDtypeStruct((2, rows, WIDTH), BF16), *outs],
        input_output_aliases={3 + len(arrays) + i: i for i in range(len(full))},
        compiler_params=pltpu.CompilerParams(vmem_limit_bytes=40 << 20),
        cost_estimate=pl.CostEstimate(
            flops=10 * CORES * blocks * slots * GROUPS * BLOCK * BLOCK * HD,
            transcendentals=CORES * blocks * slots * GROUPS * BLOCK * BLOCK,
            bytes_accessed=10 << 20,
        ),
        name="attend",
    )(
        lists.reshape(-1),
        starts,
        where,
        *[pltpu.with_memory_space_constraint(a, pltpu.HBM) for a in arrays[:2]],
        *arrays[2:],
        *full,
    )


def place_kernel(core, *refs):
    h = pl.program_id(0)
    returned, outs = refs[:PER_CORE], refs[-2:]
    for i in range(PER_CORE):

        @pl.when(h == i)
        def _():
            for kind in range(2):
                outs[kind][...] = returned[i][kind]


def place(core, returned, full):
    rows = full[0].shape[0]
    half = rows // 2
    in_spec = pl.BlockSpec((2, half, WIDTH), lambda h, i, *_: (0, i, 0))
    out_spec = pl.BlockSpec((half, WIDTH), lambda h, i, c: (i, (1 - c[0]) * PER_CORE + h))
    return pl.pallas_call(
        place_kernel,
        grid_spec=pltpu.PrefetchScalarGridSpec(
            num_scalar_prefetch=1,
            grid=(PER_CORE, 2),
            in_specs=[in_spec] * PER_CORE + [ANY] * 2,
            out_specs=[out_spec] * 2,
        ),
        out_shape=[jax.ShapeDtypeStruct(f.shape, f.dtype) for f in full],
        input_output_aliases={1 + PER_CORE + i: i for i in range(2)},
        compiler_params=SMALL,
        name="place",
    )(core, *returned, *full)


def total_kernel(chip_part, back, own, other):
    rows = own.shape[1]
    for kind, scale in enumerate((SCALING, 1.0)):
        total = (chip_part[kind] * scale + back[kind].astype(F32)).astype(BF16)
        own[kind] = total[:rows]
        other[kind] = total[rows:]


def total(chip_part, back):
    rows = chip_part.shape[1] // CORES
    return pl.pallas_call(
        total_kernel,
        out_shape=[jax.ShapeDtypeStruct((2, rows, HD), BF16)] * CORES,
        compiler_params=SMALL,
        name="total",
    )(chip_part, back)


def early_kernel(core, *refs):
    outs = refs[-2:]
    for h in range(PER_CORE - 1):
        for which, owner in enumerate((core[0], 1 - core[0])):
            at = columns(owner * PER_CORE + h, HD)
            for kind in range(2):
                outs[kind][:, at] = refs[CORES * h + which][kind]


def early_grads(core, pieces):
    rows = pieces[0].shape[1]
    strip = pl.BlockSpec((2, rows, HD), lambda i, *_: (0, 0, 0))
    out = pl.BlockSpec((rows, KV_HEADS * HD), lambda i, *_: (0, 0))
    return pl.pallas_call(
        early_kernel,
        grid_spec=pltpu.PrefetchScalarGridSpec(
            num_scalar_prefetch=1,
            grid=(1,),
            in_specs=[strip] * len(pieces),
            out_specs=[out, out],
        ),
        out_shape=[jax.ShapeDtypeStruct((rows, KV_HEADS * HD), BF16)] * 2,
        compiler_params=SMALL,
        name="early_grads",
    )(core, *pieces)


def last_kernel(core, own_part, own_back, other_part, other_back, before_k, before_v, *outs):
    step = pl.program_id(0)

    @pl.when(step == 0)
    def _():
        for kind, scale in enumerate((SCALING, 1.0)):
            value = own_part[kind] * scale + own_back[kind].astype(F32)
            outs[kind][...] = value.astype(BF16)

    @pl.when(step == 1)
    def _():
        for kind in range(2):
            value = other_part[kind].astype(F32) + other_back[kind].astype(F32)
            outs[kind][...] = value.astype(BF16)


def last_grads(core, pieces, early):
    rows = pieces[0].shape[1]
    strip = pl.BlockSpec((2, rows, HD), lambda i, *_: (0, 0, 0))

    def place_of(step, core):
        owner = core[0] + step * (1 - 2 * core[0])
        return 0, owner * PER_CORE + PER_CORE - 1

    out = pl.BlockSpec((rows, HD), place_of)
    return pl.pallas_call(
        last_kernel,
        grid_spec=pltpu.PrefetchScalarGridSpec(
            num_scalar_prefetch=1,
            grid=(CORES,),
            in_specs=[strip] * len(pieces) + [ANY] * 2,
            out_specs=[out, out],
        ),
        out_shape=[jax.ShapeDtypeStruct(e.shape, e.dtype) for e in early],
        input_output_aliases={1 + len(pieces) + i: i for i in range(2)},
        compiler_params=SMALL,
        name="last_grads",
    )(core, *pieces, *early)


def per_device(queries, keys, values, out_grad, doc_starts, block_lists):
    device = lax.axis_index("ctx").astype(jnp.int32)
    count = lax.axis_size("ctx")
    core = lax.rem(device, CORES).reshape(1)
    where = device.reshape(1)
    chips = count // CORES

    pairs = [(2 * c + k, 2 * c + 1 - k) for c in range(chips) for k in range(CORES)]
    same = [(2 * c + k, 2 * c + 2 + k) for c in range(chips - 1) for k in range(CORES)]
    cross = [(2 * c + k, 2 * c + 3 - k) for c in range(chips - 1) for k in range(CORES)]
    same_back = [(b, a) for a, b in same]
    cross_back = [(b, a) for a, b in cross]

    def send(value, route):
        return lax.ppermute(value, "ctx", route)

    packed = pack(core, keys, values)
    own, other, sib, prev = packed[0::CORES], packed[1::CORES], [], []
    for h in range(PER_CORE):
        mine, theirs = own[h], other[h]
        sib.append(send(theirs, pairs))
        if h == 0:
            prev.append([send(mine, same), send(theirs, cross)])
        else:
            prev.append([send(jnp.concatenate([mine, sib[h]], axis=1), same)])
    late, _ = lax.optimization_barrier(((queries, out_grad, block_lists), packed))
    sib_queries, sib_out_grad, sib_lists = [send(value, pairs) for value in late]
    lists = jnp.concatenate([block_lists, sib_lists])

    full, returned, pieces, back = (), [], [], None
    for h in range(PER_CORE):
        last = h == PER_CORE - 1
        parts = [(1, F32)] + [(1, BF16)] * 3 if last else [(CORES, F32), (CORES, BF16)]
        arrays = (queries, out_grad, sib_queries, sib_out_grad, own[h], sib[h], *prev[h])
        att, dq, to_sibling, *parts = attend(h, lists, doc_starts, where, arrays, full, parts)
        full = (att, dq)
        if h > 0:
            to_sibling, parts, back = lax.optimization_barrier((to_sibling, parts, back))
            own_total, other_total = total(chip_part, back)
            pieces += [own_total, send(other_total, pairs)]
        returned.append(send(to_sibling, pairs))
        if not last:
            chip_part, to_prev = parts
            back = send(to_prev, same_back)
        else:
            own_part, sib_part, to_same, to_cross = parts
            own_back, other_back = send(to_same, same_back), send(to_cross, cross_back)
            other_part = send(sib_part, pairs)
    attended, grad_query = place(core, returned, full)
    early = early_grads(core, pieces)
    attended, grad_query, early, other_back = lax.optimization_barrier(
        (attended, grad_query, early, other_back)
    )
    last_pieces = (own_part, own_back, other_part, other_back)
    return attended, grad_query, *last_grads(core, last_pieces, early)


def solution(mesh):
    tokens = P(("grp", "ctx"), None)
    return jax.shard_map(
        per_device,
        mesh=mesh,
        in_specs=(tokens, tokens, tokens, tokens, P("grp"), tokens),
        out_specs=(tokens, tokens, tokens, tokens),
        check_vma=False,
    )
```
